256 devices in a mesh: row: 16 (over z, x_hi), col: 16 (over y, x_lo, core).
Axes of the slice: x: 4 (x_hi: 2, x_lo: 2; x = x_hi * 2 + x_lo), y: 4, z: 8, core: 2. Of those that a mesh axis runs over, the one named last changes fastest.
Arguments:
- front_base: float32 [8, 16, 128, 8, 16, 128], P(None, 'row', None, None, 'col')
- traces: bfloat16 [8, 16, 4, 3, 128, 128], P(None, 'row'), may hold values from -0.75 to 0.75
- adjacency: int32 [128, 4], replicated, may hold values from 0 to 127, as said below
- pivot_order: int32 [2, 512], replicated, may hold values from 0 to 511, each once within a row
- pivot_kind: int32 [2, 512], replicated, may hold values from 0 to 2, as said below
- inverse_diagonal: float32 [2, 512], replicated, may hold values from -0.3 to 0.3
- inverse_coupling: float32 [2, 512], replicated, may hold values from -0.3 to 0.3
- readers: int32 [2, 128], replicated, may hold values 0 or 1
Outputs:
- trailing: float32 [8, 16, 128, 8, 16, 128], P(None, 'row', None, None, 'col')
The draws below stay inside these ranges and needn't reach their ends.
Inputs may be any that keep to these rules, and one draw needn't show every extreme that they name: The elements form a 16 x 8 grid that closes on itself in both dimensions, numbered in a drawn order; faces 0 and 1 lead to the next and previous element along the first dimension, 2 and 3 along the second, so adjacency[adjacency[e, f], f with its lowest bit flipped] = e. `pivot_kind`: 0 marks a 1 x 1 pivot; 1 marks the first position of a 2 x 2 pivot, whose second position follows and is marked 2; 2 x 2 pivots start at even positions.
All inputs are finite; a program needn't handle non-finite values.
Results may differ from the reference program's by a relative error of at most 0.008.
Values may be sent and summed in bfloat16 or wider, within the bound.
No kernel may reach another device: no remote copies, remote signals or barrier semaphores. Data moves between devices by JAX's collectives and lax.ppermute only.
A program may use at most 128 MiB of HBM per device.

```python
import jax
import jax.numpy as jnp

NB = 128
Q = 128
E = 128
EGY = 8
PW = 512
PANELS = 2
RB = 8
N_ROW = 16
N_COL = 16


def draw_front_base(key, part):
    front_order = E * NB
    entries = jax.random.normal(key, (front_order, front_order), jnp.float32)
    symmetric = (entries + entries.T) * 0.7071
    return symmetric.reshape(E // N_ROW, N_ROW, NB, E // N_COL, N_COL, NB)


def draw_adjacency(key, part):
    element_ids = jax.random.permutation(key, E).astype(jnp.int32)
    element_grid = element_ids.reshape(E // EGY, EGY)
    neighbours = jnp.stack([jnp.roll(element_grid, -1, 0), jnp.roll(element_grid, 1, 0), jnp.roll(element_grid, -1, 1), jnp.roll(element_grid, 1, 1)], axis=-1).reshape(E, 4)
    return jnp.zeros((E, 4), jnp.int32).at[element_grid.reshape(E)].set(neighbours)


def draw_pivot_kind(key, part):
    pair_flags = jax.random.randint(key, (PANELS, PW // 2), 0, 2).astype(jnp.int32)
    return jnp.stack([pair_flags, 2 * pair_flags], axis=-1).reshape(PANELS, PW)


def plant(values, rng, low, high):
    extent = values.shape
    index_at = [jax.random.randint(jax.random.fold_in(rng, axis), (), 0, extent[axis]) for axis in range(len(extent))]
    values = values.at[tuple(index_at)].set(low)
    longest = extent.index(max(extent))
    index_at[longest] = (index_at[longest] + 1) % extent[longest]
    return values.at[tuple(index_at)].set(high)


def steps_of(rng, extent, split, low, high):
    loudness, own = 1.0, jax.random.fold_in(rng, 6)
    for dim, blocks in split:
        heights = jnp.exp(jax.random.uniform(jax.random.fold_in(own, dim), (blocks,), jnp.float32, low / len(split), high / len(split)))
        loudness = loudness * jnp.repeat(heights, extent[dim] // blocks).reshape([-1 if axis == dim else 1 for axis in range(len(extent))])
    return loudness


def centred(rng, shape, deviation, limit, pieces=(), kind=jnp.bfloat16):
    drawn = deviation * jax.random.normal(rng, shape, jnp.float32)
    if pieces:
        drawn = drawn * steps_of(rng, shape, pieces, -0.22, 0.18)
    return jnp.clip(drawn, -limit, limit).astype(kind)


def setup_inputs(seed: int = 0) -> dict:
    seeds = jax.random.split(jax.random.key(seed), 9)
    front_base = draw_front_base(jax.random.fold_in(seeds[8], 71), 0)
    traces = centred(seeds[1], (RB, N_ROW, 4, 3, Q, NB), 0.125, 0.75, ((1, 16),))
    adjacency = draw_adjacency(jax.random.fold_in(seeds[8], 71), 0)
    pivot_order = jax.vmap(lambda own: jax.random.permutation(own, PW))(jax.random.split(seeds[3], PANELS)).reshape((PANELS, PW)).astype(jnp.int32)
    pivot_kind = draw_pivot_kind(jax.random.fold_in(seeds[8], 71), 0)
    inverse_diagonal = centred(seeds[5], (PANELS, PW), 0.05, 0.3, (), jnp.float32)
    inverse_coupling = centred(seeds[6], (PANELS, PW), 0.05, 0.3, (), jnp.float32)
    readers = plant((jax.random.randint(seeds[7], (PANELS, E), 0, 4) < 3).astype(jnp.int32), jax.random.fold_in(seeds[7], 1), 0, 1)
    return {"front_base": front_base, "traces": traces, "adjacency": adjacency, "pivot_order": pivot_order, "pivot_kind": pivot_kind, "inverse_diagonal": inverse_diagonal, "inverse_coupling": inverse_coupling, "readers": readers}


def face_left(values):
    return jnp.concatenate([values[:, :, 0], values[:, :, 0], values[:, :, 1], values[:, :, 2]], axis=2)


def face_right(values):
    return jnp.concatenate([4.0 * values[:, :, 0], -0.5 * values[:, :, 1], -0.5 * values[:, :, 0], 2.0 * values[:, :, 2]], axis=2)


def apply_inverse(values, pivot_kinds, diagonal, pair_terms):
    starts = (pivot_kinds == 1).astype(values.dtype)
    upward = pair_terms * starts
    upward_prev = jnp.concatenate([jnp.zeros_like(upward[:1]), upward[:-1]])
    following = jnp.concatenate([values[:, 1:], jnp.zeros_like(values[:, :1])], axis=1)
    preceding = jnp.concatenate([jnp.zeros_like(values[:, :1]), values[:, :-1]], axis=1)
    return values * diagonal + following * upward + preceding * upward_prev


def reference(front_base, traces, adjacency, pivot_order, pivot_kind, inverse_diagonal, inverse_coupling, readers):
    front_order = E * NB
    element_traces = traces.reshape(E, 4, 3, Q, NB)
    left_parts = face_left(element_traces).astype(jnp.float32)
    right_parts = face_right(element_traces).astype(jnp.float32)
    opposite = jnp.array([1, 0, 3, 2], dtype=jnp.int32)
    partner = right_parts[adjacency, opposite[None, :]]
    coupling = jnp.einsum("efqi,efqj->efij", left_parts, partner)
    self_terms = jnp.einsum("efqi,efqj->eij", left_parts, right_parts)
    blocks = front_base.reshape(E, NB, E, NB)
    rows_index = jnp.broadcast_to(jnp.arange(E, dtype=jnp.int32)[:, None], (E, 4))
    blocks = blocks.at[rows_index, :, adjacency, :].add(-coupling)
    diag_index = jnp.arange(E, dtype=jnp.int32)
    blocks = blocks.at[diag_index, :, diag_index, :].add(self_terms)
    front_mat = blocks.reshape(front_order, front_order)
    block_id = jnp.arange(E, dtype=jnp.int32)
    for which_panel in range(PANELS):
        first_col = which_panel * PW
        columns = front_mat[:, first_col:first_col + PW].astype(jnp.bfloat16)
        columns = jnp.take(columns, pivot_order[which_panel], axis=1)
        kept_blocks = readers[which_panel] * (block_id >= (first_col + PW) // NB).astype(jnp.int32)
        kept_rows = jnp.repeat(kept_blocks, NB).astype(jnp.bfloat16)
        panel_vals = columns * kept_rows[:, None]
        scaled = apply_inverse(panel_vals.astype(jnp.float32), pivot_kind[which_panel], inverse_diagonal[which_panel], inverse_coupling[which_panel]).astype(jnp.bfloat16)
        front_mat = front_mat - jnp.dot(scaled, panel_vals.T, preferred_element_type=jnp.float32)
    return front_mat.reshape(E // N_ROW, N_ROW, NB, E // N_COL, N_COL, NB)
```

```python
import jax
import jax.numpy as jnp
from jax import lax
from jax.experimental import pallas as pl
from jax.experimental.pallas import tpu as pltpu
from jax.sharding import PartitionSpec as P

NB = 128
PW = 512
N = 16
BOTH = ("row", "col")
F32 = jnp.float32
BF16 = jnp.bfloat16

SWAP_X = [(r, r ^ 1) for r in range(N)]
Z_LINES = [[2 * z + x for z in range(8)] for x in (0, 1)]


def spread_target(q, j):
    return 2 * ((q // 2 + j // 2) % 8) + j % 2


SPREAD = [(q * N + j, spread_target(q, j) * N + q) for q in range(N) for j in range(N)]
SPREAD_LOW = [(s, d) for s, d in SPREAD if s // N < 8]
HALVE = [(n, n + 8) for n in range(8)]


def left_of(ref, lead):
    v, s, l = ref[lead + (0,)], ref[lead + (1,)], ref[lead + (2,)]
    return jnp.concatenate([v, v, s, l], axis=0)


def right_of(ref, lead):
    v, s, l = ref[lead + (0,)], ref[lead + (1,)], ref[lead + (2,)]
    return jnp.concatenate([v * 4.0, s * -0.5, v * -0.5, l * 2.0], axis=0).astype(BF16)


def pair_product(left, right):
    return lax.dot_general(left, right, (((0,), (0,)), ((), ())), preferred_element_type=F32)


def panel_block_kernel(place, adj, base, own, faces, out, acc):
    r, c = place[0], place[1]
    acc[...] = base[...]
    for g in range(4):
        e = adj[c * 4 + g]

        @pl.when((e % N == r) & (c < 8))
        def _():
            a = e // N
            acc[a] -= pair_product(left_of(own, (a, g ^ 1)), right_of(faces, (g,)))

    @pl.when(r == c)
    def _():
        for f in range(4):
            acc[0] += pair_product(left_of(own, (0, f)), right_of(own, (0, f)))

    out[...] = acc[...].astype(BF16)


def assemble_kernel(place, adj, base, own, faces, out):
    r, c = place[0], place[1]
    a = pl.program_id(0)
    out[...] = base[...]
    for f in range(4):
        n = adj[(a * N + r) * 4 + f]

        @pl.when(n % N == c)
        def _():
            g = f ^ 1
            b = n // N
            right = right_of(faces, (b, (g // 2) ^ (r % 2), g % 2))
            rows = pl.ds(b, NB, stride=8)
            out[0, rows, :] = out[0, rows, :] - pair_product(left_of(own, (0, f)), right)

    @pl.when(r == c)
    def _():
        total = pair_product(left_of(own, (0, 0)), right_of(own, (0, 0)))
        for f in range(1, 4):
            total += pair_product(left_of(own, (0, f)), right_of(own, (0, f)))
        rows = pl.ds(a, NB, stride=8)
        out[0, rows, :] = out[0, rows, :] + total


def dot_nt(x, y):
    return lax.dot_general(x, y, (((1,), (1,)), ((), ())), preferred_element_type=F32)


def scale(values, partner, diag, side):
    swapped = jnp.dot(values, partner, preferred_element_type=F32)
    return (values.astype(F32) * diag + swapped * side).astype(BF16)


def keep(readers, k, e):
    return jnp.where((readers[k * 128 + e] == 1) & (e >= 4 * (k + 1)), 1.0, 0.0).astype(F32)


def update_kernel(
    place, readers, front, row_half, col_half, cross, partner, diag, side, out,
    v0c, v1c, cross_t, v0r, f1r,
):
    r, c = place[0], place[1]
    step = pl.program_id(0)

    @pl.when(step == 0)
    def _():
        for i in range(4):
            kept = keep(readers, 0, 4 + i)
            for n in range(4):
                for s in range(4):
                    tile = cross[4 * n + s, i].astype(F32) * kept
                    cross_t[i * NB + s * 32 : i * NB + (s + 1) * 32, n * NB : (n + 1) * NB] = tile.astype(BF16)
        for b in range(8):
            e = b * N + c
            kept = keep(readers, 0, e)
            for n in range(8):
                j = n + 8 * (b // 4)
                tile = col_half[(j // 2 + c // 2) % 8, (j % 2) ^ (r % 2), b % 4]
                rows = slice(b * NB, (b + 1) * NB)
                if n < 4:
                    v0c[rows, n * NB : (n + 1) * NB] = (tile.astype(F32) * kept).astype(BF16)
                else:
                    v1c[rows, (n - 4) * NB : (n - 3) * NB] = tile
        w0c = scale(v0c[...], partner[0], diag[0:1], side[0:1])
        fresh = v1c[...].astype(F32) - dot_nt(w0c, cross_t[...])
        for b in range(8):
            kept = keep(readers, 1, b * N + c)
            v1c[b * NB : (b + 1) * NB, :] = (fresh[b * NB : (b + 1) * NB] * kept).astype(BF16)

    for t in range(2):
        a = 2 * step + t
        kept = keep(readers, 0, a * N + r)
        rows = slice(t * NB, (t + 1) * NB)
        for n in range(8):
            tile = row_half[n + 8 * (a // 4), a % 4]
            if n < 4:
                v0r[rows, n * NB : (n + 1) * NB] = (tile.astype(F32) * kept).astype(BF16)
            else:
                f1r[rows, (n - 4) * NB : (n - 3) * NB] = tile
    w0r = scale(v0r[...], partner[0], diag[0:1], side[0:1])
    fresh = f1r[...].astype(F32) - dot_nt(w0r, cross_t[...])
    for t in range(2):
        kept = keep(readers, 1, (2 * step + t) * N + r)
        f1r[t * NB : (t + 1) * NB, :] = (fresh[t * NB : (t + 1) * NB] * kept).astype(BF16)
    w1r = scale(f1r[...], partner[1], diag[1:2], side[1:2])
    change = dot_nt(w0r, v0c[...]) + dot_nt(w1r, v1c[...])
    for t in range(2):
        for b in range(8):
            rows = pl.ds(b, NB, stride=8)
            out[t, rows, :] = front[t, rows, :] - change[t * NB : (t + 1) * NB, b * NB : (b + 1) * NB]


def pivot_tables(pivot_order, pivot_kind, inverse_diagonal, inverse_coupling):
    at = pivot_order[:, :, None] == jnp.arange(PW, dtype=jnp.int32)[None, None, :]
    starts = jnp.where(pivot_kind == 1, inverse_coupling, 0.0).reshape(2, PW // 2, 2)[:, :, 0]
    factor = jnp.repeat(starts, 2, axis=1)
    diag = jnp.sum(jnp.where(at, inverse_diagonal[:, :, None], 0.0), axis=1)
    side = jnp.sum(jnp.where(at, factor[:, :, None], 0.0), axis=1)
    order_swapped = pivot_order.reshape(2, PW // 2, 2)[:, :, ::-1].reshape(2, PW)
    partner_of = jnp.sum(jnp.where(at, order_swapped[:, :, None], 0), axis=1)
    partner = (jnp.arange(PW, dtype=jnp.int32)[None, :, None] == partner_of[:, None, :]).astype(BF16)
    return partner, diag, side


def smem():
    return pl.BlockSpec(memory_space=pltpu.SMEM)


def vmem():
    return pl.BlockSpec(memory_space=pltpu.VMEM)


def local(
    front_base, traces, adjacency, pivot_order, pivot_kind, inverse_diagonal, inverse_coupling, readers,
):
    r = lax.axis_index("row")
    c = lax.axis_index("col")
    place = jnp.stack([r, c]).astype(jnp.int32)
    adj = adjacency.reshape(-1)
    own = traces[:, 0]
    base = front_base.reshape(8, 8 * NB, NB)

    low_faces = lax.ppermute(own[0], BOTH, SPREAD_LOW)

    target = 2 * ((r // 2 + c // 2) % 8) + c % 2
    piece = lax.dynamic_slice_in_dim(own.reshape(32, 3, NB, NB), 2 * target, 2, axis=0)
    piece = lax.ppermute(piece, BOTH, SPREAD)
    both = jnp.stack([piece, lax.ppermute(piece, "row", SWAP_X)])
    faces = lax.all_gather(both, "row", axis=0, axis_index_groups=Z_LINES)

    base_low = front_base[:, 0, :, 0, 0, :]
    block = pl.pallas_call(
        panel_block_kernel,
        out_shape=jax.ShapeDtypeStruct((8, NB, NB), BF16),
        in_specs=[smem(), smem(), vmem(), vmem(), vmem()],
        out_specs=vmem(),
        scratch_shapes=[pltpu.VMEM((8, NB, NB), F32)],
        name="panel_block",
    )(place, adj, base_low, own, low_faces)
    upper = lax.ppermute(block[4:], "col", HALVE)
    half = jnp.where(c < 8, block[:4], upper)

    spread = lax.ppermute(half, BOTH, SPREAD)
    pair = jnp.stack([spread, lax.ppermute(spread, "row", SWAP_X)])
    col_half = lax.all_gather(pair, "row", axis=0, axis_index_groups=Z_LINES)

    row_half = lax.all_to_all(jnp.broadcast_to(half[None], (N,) + half.shape), "col", 0, 0, tiled=True)

    first = row_half[:4, 0].reshape(N, 32, NB)
    part = lax.dynamic_index_in_dim(first, c, 0, keepdims=False)
    part = lax.all_to_all(jnp.broadcast_to(part[None], (N, 32, NB)), "row", 0, 0, tiled=True)[4:8]
    cross = lax.all_to_all(jnp.broadcast_to(part[None], (N, 4, 32, NB)), "col", 0, 0, tiled=True)

    partner, diag, side = pivot_tables(pivot_order, pivot_kind, inverse_diagonal, inverse_coupling)

    front = pl.pallas_call(
        assemble_kernel,
        grid=(8,),
        out_shape=jax.ShapeDtypeStruct((8, 8 * NB, NB), F32),
        in_specs=[
            smem(),
            smem(),
            pl.BlockSpec((1, 8 * NB, NB), lambda a: (a, 0, 0)),
            pl.BlockSpec((1, 4, 3, NB, NB), lambda a: (a, 0, 0, 0, 0)),
            vmem(),
        ],
        out_specs=pl.BlockSpec((1, 8 * NB, NB), lambda a: (a, 0, 0)),
        name="assemble",
    )(place, adj, base, own, faces)

    out = pl.pallas_call(
        update_kernel,
        grid=(4,),
        out_shape=jax.ShapeDtypeStruct((8, 8 * NB, NB), F32),
        in_specs=[
            smem(),
            smem(),
            pl.BlockSpec((2, 8 * NB, NB), lambda s: (s, 0, 0)),
            vmem(),
            vmem(),
            vmem(),
            vmem(),
            vmem(),
            vmem(),
        ],
        out_specs=pl.BlockSpec((2, 8 * NB, NB), lambda s: (s, 0, 0)),
        scratch_shapes=[
            pltpu.VMEM((8 * NB, PW), BF16),
            pltpu.VMEM((8 * NB, PW), BF16),
            pltpu.VMEM((PW, PW), BF16),
            pltpu.VMEM((2 * NB, PW), BF16),
            pltpu.VMEM((2 * NB, PW), BF16),
        ],
        name="update",
    )(place, readers.reshape(-1), front, row_half, col_half, cross, partner, diag, side)
    return out.reshape(8, 1, NB, 8, 1, NB)


def solution(mesh):
    in_specs = (
        P(None, "row", None, None, "col", None),
        P(None, "row", None, None, None, None),
        P(),
        P(),
        P(),
        P(),
        P(),
        P(),
    )
    out_specs = P(None, "row", None, None, "col", None)
    return jax.shard_map(local, mesh=mesh, in_specs=in_specs, out_specs=out_specs, check_vma=False)
```

```python
import jax
import jax.numpy as jnp
from jax import lax
from jax.experimental import pallas as pl
from jax.experimental.pallas import tpu as pltpu
from jax.sharding import PartitionSpec as P


NB = 128
PW = 512
N = 16
BOTH = ("row", "col")
F32 = jnp.float32
BF16 = jnp.bfloat16

SWAP_X = [(r, r ^ 1) for r in range(N)]
Z_LINES = [[2 * z + x for z in range(8)] for x in (0, 1)]


def spread_target(q, j):
    return 2 * ((q // 2 + j // 2) % 8) + j % 2


SPREAD = [(q * N + j, spread_target(q, j) * N + q) for q in range(N) for j in range(N)]
SPREAD_A = [(s, d) for s, d in SPREAD if s % N < 8]
SPREAD_B = [(s - 8, d) for s, d in SPREAD if s % N >= 8]
HALVE = [(n, n + 8) for n in range(8)]
SWAP_CORE = [(c, c ^ 1) for c in range(N)]
SAME_CORE = [[2 * i + k for i in range(8)] for k in (0, 1)]


def left_of(ref, lead):
    v, s, l = ref[lead + (0,)], ref[lead + (1,)], ref[lead + (2,)]
    return jnp.concatenate([v, v, s, l], axis=0)


def right_of_parts(v, s, l):
    return jnp.concatenate([v * 4.0, s * -0.5, v * -0.5, l * 2.0], axis=0).astype(BF16)


def right_of(ref, lead):
    return right_of_parts(ref[lead + (0,)], ref[lead + (1,)], ref[lead + (2,)])


def right_of_chunks(chunks):
    rows = jnp.concatenate(chunks, axis=0)
    return right_of_parts(rows[:NB], rows[NB : 2 * NB], rows[2 * NB :])


def pair_product(left, right):
    return lax.dot_general(left, right, (((0,), (0,)), ((), ())), preferred_element_type=F32)


def panel_block_kernel(place, adj, base, own, faces, lower, upper, acc):
    r, c = place[0], place[1]
    acc[...] = base[...]
    for g in range(4):
        e = adj[c * 4 + g]

        @pl.when((e % N == r) & (c < 8))
        def _():
            a = e // N
            right = right_of_chunks([faces[2 * (4 * (g % 2) + k) + g // 2] for k in range(4)])
            acc[a] -= pair_product(left_of(own, (a, g ^ 1)), right)

    @pl.when(r == c)
    def _():
        for f in range(4):
            acc[0] += pair_product(left_of(own, (0, f)), right_of(own, (0, f)))

    lower[...] = acc[:4].astype(BF16)
    upper[...] = acc[4:].astype(BF16)


def couple(place, adj, own, faces, out, t, a, parity):
    r, c = place[0], place[1]
    for f in (0, 1) if parity == 0 else (2, 3):
        n = adj[(a * N + r) * 4 + f]

        @pl.when(n % N == c)
        def _():
            b = n // N
            right = right_of_chunks([faces[4 * (1 - f % 2) + k, b] for k in range(4)])
            rows = pl.ds(b, NB, stride=8)
            out[t, rows, :] = out[t, rows, :] - pair_product(left_of(own, (t, f)), right)


def assemble_kernel(place, adj, base, own, faces, out):
    r, c = place[0], place[1]
    a = pl.program_id(0)
    out[...] = base[...]
    for parity in (0, 1):
        pl.when(r % 2 == parity)(lambda: couple(place, adj, own, faces, out, 0, a, parity))

    @pl.when(r == c)
    def _():
        total = pair_product(left_of(own, (0, 0)), right_of(own, (0, 0)))
        for f in range(1, 4):
            total += pair_product(left_of(own, (0, f)), right_of(own, (0, f)))
        rows = pl.ds(a, NB, stride=8)
        out[0, rows, :] = out[0, rows, :] + total


def dot_nt(x, y):
    return lax.dot_general(x, y, (((1,), (1,)), ((), ())), preferred_element_type=F32)


def scale(values, partner, diag, side):
    swapped = jnp.dot(values, partner, preferred_element_type=F32)
    return (values.astype(F32) * diag + swapped * side).astype(BF16)


def keep(readers, k, e):
    return jnp.where((readers[k * 128 + e] == 1) & (e >= 4 * (k + 1)), 1.0, 0.0).astype(F32)


def row_side_kernel(place, readers, row_own, row_other, partner, diag, side, w0r, w1r, cross, v0r, f1r):
    r, c = place[0], place[1]
    step = pl.program_id(0)

    def tile_of(n, chunk, slot):
        at = (n // 2 + 4 * chunk, slot)
        return jnp.where(c % 2 == n % 2, row_own[at], row_other[at])

    @pl.when(step == 0)
    def _():
        for i in range(4):
            kept = keep(readers, 0, 4 + i)
            for n in range(4):
                tile = tile_of(n, i // 2, 4 + i % 2).astype(F32) * kept
                cross[i * NB : (i + 1) * NB, n * NB : (n + 1) * NB] = tile.astype(BF16)

    for t in range(2):
        a = 2 * step + t
        kept = keep(readers, 0, a * N + r)
        rows = slice(t * NB, (t + 1) * NB)
        for n in range(8):
            tile = tile_of(n, a // 4, a % 4)
            if n < 4:
                v0r[rows, n * NB : (n + 1) * NB] = (tile.astype(F32) * kept).astype(BF16)
            else:
                f1r[rows, (n - 4) * NB : (n - 3) * NB] = tile
    w0 = scale(v0r[...], partner[0], diag[0:1], side[0:1])
    w0r[...] = w0
    fresh = f1r[...].astype(F32) - dot_nt(w0, cross[...])
    for t in range(2):
        kept = keep(readers, 1, (2 * step + t) * N + r)
        f1r[t * NB : (t + 1) * NB, :] = (fresh[t * NB : (t + 1) * NB] * kept).astype(BF16)
    w1r[...] = scale(f1r[...], partner[1], diag[1:2], side[1:2])


def update_kernel(
    place, adj, readers, front, own, faces_x, w0r, w1r, cross, col_half, partner, diag, side, out, v0c, v1c,
):
    r, c = place[0], place[1]
    step = pl.program_id(0)

    @pl.when(step == 0)
    def _():
        for b in range(8):
            kept = keep(readers, 0, b * N + c)
            for n in range(8):
                j = n + 8 * (b // 4)
                tile = col_half[(j // 2 + c // 2) % 8, (j % 2) ^ (r % 2), b % 4]
                rows = slice(b * NB, (b + 1) * NB)
                if n < 4:
                    v0c[rows, n * NB : (n + 1) * NB] = (tile.astype(F32) * kept).astype(BF16)
                else:
                    v1c[rows, (n - 4) * NB : (n - 3) * NB] = tile
        w0c = scale(v0c[...], partner[0], diag[0:1], side[0:1])
        fresh = v1c[...].astype(F32) - dot_nt(w0c, cross[...])
        for b in range(8):
            kept = keep(readers, 1, b * N + c)
            v1c[b * NB : (b + 1) * NB, :] = (fresh[b * NB : (b + 1) * NB] * kept).astype(BF16)

    change = dot_nt(w0r[...], v0c[...]) + dot_nt(w1r[...], v1c[...])
    for t in range(2):
        for b in range(8):
            rows = pl.ds(b, NB, stride=8)
            out[t, rows, :] = front[t, rows, :] - change[t * NB : (t + 1) * NB, b * NB : (b + 1) * NB]
        for parity in (0, 1):
            pl.when(r % 2 != parity)(lambda: couple(place, adj, own, faces_x, out, t, 2 * step + t, parity))


def pivot_tables(pivot_order, pivot_kind, inverse_diagonal, inverse_coupling):
    at = pivot_order[:, :, None] == jnp.arange(PW, dtype=jnp.int32)[None, None, :]
    starts = jnp.where(pivot_kind == 1, inverse_coupling, 0.0).reshape(2, PW // 2, 2)[:, :, 0]
    factor = jnp.repeat(starts, 2, axis=1)
    diag = jnp.sum(jnp.where(at, inverse_diagonal[:, :, None], 0.0), axis=1)
    side = jnp.sum(jnp.where(at, factor[:, :, None], 0.0), axis=1)
    order_swapped = pivot_order.reshape(2, PW // 2, 2)[:, :, ::-1].reshape(2, PW)
    partner_of = jnp.sum(jnp.where(at, order_swapped[:, :, None], 0), axis=1)
    partner = (jnp.arange(PW, dtype=jnp.int32)[None, :, None] == partner_of[:, None, :]).astype(BF16)
    return partner, diag, side


def smem():
    return pl.BlockSpec(memory_space=pltpu.SMEM)


def vmem():
    return pl.BlockSpec(memory_space=pltpu.VMEM)


def steps(
    front_base, traces, adjacency, pivot_order, pivot_kind, inverse_diagonal, inverse_coupling, readers,
):
    r = lax.axis_index("row")
    c = lax.axis_index("col")
    place = jnp.stack([r, c]).astype(jnp.int32)
    adj = adjacency.reshape(-1)
    own = traces[:, 0]
    base = front_base.reshape(8, 8 * NB, NB)

    chunk = (r // 2 + c // 2) % 8 + 8 * (c % 2)
    piece = lax.dynamic_index_in_dim(own.reshape(8, N, 96, NB), chunk, 1, keepdims=False)
    piece = lax.ppermute(piece, BOTH, SPREAD)
    faces = lax.all_gather(piece, "row", axis=0, axis_index_groups=Z_LINES)
    faces_x = lax.ppermute(faces, "row", SWAP_X)
    low_faces = lax.all_to_all(jnp.broadcast_to(piece[:1], (N, 96, NB)), "row", 0, 0, tiled=True)

    base_low = front_base[:, 0, :, 0, 0, :]
    lower, upper = pl.pallas_call(
        panel_block_kernel,
        out_shape=(jax.ShapeDtypeStruct((4, NB, NB), BF16),) * 2,
        in_specs=[smem(), smem(), vmem(), vmem(), vmem()],
        out_specs=(vmem(), vmem()),
        scratch_shapes=[pltpu.VMEM((8, NB, NB), F32)],
        name="panel_block",
    )(place, adj, base_low, own, low_faces)

    spread_a = lax.ppermute(lower, BOTH, SPREAD_A)
    spread_b = lax.ppermute(upper, BOTH, SPREAD_B)
    spread = jnp.where((r // 2 - c // 2) % 8 < 4, spread_a, spread_b)
    other = lax.ppermute(spread, "row", SWAP_X)
    pair = jnp.stack([spread, other])
    col_half = lax.all_gather(pair, "row", axis=0, axis_index_groups=Z_LINES)

    cross_row = lax.all_to_all(jnp.broadcast_to(lower[:1], (N, NB, NB)), "row", 0, 0, tiled=True)[4:8]

    moved = lax.ppermute(jnp.concatenate([upper, cross_row[2:]]), "col", HALVE)
    half = jnp.where(c < 8, jnp.concatenate([lower, cross_row[:2]]), moved)
    row_own = lax.all_to_all(
        jnp.broadcast_to(half[None], (8,) + half.shape), "col", 0, 0, tiled=True, axis_index_groups=SAME_CORE
    )
    row_other = lax.ppermute(row_own, "col", SWAP_CORE)

    partner, diag, side = pivot_tables(pivot_order, pivot_kind, inverse_diagonal, inverse_coupling)

    front = pl.pallas_call(
        assemble_kernel,
        grid=(8,),
        out_shape=jax.ShapeDtypeStruct((8, 8 * NB, NB), F32),
        in_specs=[
            smem(),
            smem(),
            pl.BlockSpec((1, 8 * NB, NB), lambda a: (a, 0, 0)),
            pl.BlockSpec((1, 4, 3, NB, NB), lambda a: (a, 0, 0, 0, 0)),
            vmem(),
        ],
        out_specs=pl.BlockSpec((1, 8 * NB, NB), lambda a: (a, 0, 0)),
        name="assemble",
    )(place, adj, base, own, faces)

    by_two = pl.BlockSpec((2 * NB, PW), lambda s: (s, 0))
    w0r, w1r, cross = pl.pallas_call(
        row_side_kernel,
        grid=(4,),
        out_shape=(jax.ShapeDtypeStruct((8 * NB, PW), BF16),) * 2 + (jax.ShapeDtypeStruct((PW, PW), BF16),),
        in_specs=[smem(), smem(), vmem(), vmem(), vmem(), vmem(), vmem()],
        out_specs=(by_two, by_two, pl.BlockSpec((PW, PW), lambda s: (0, 0))),
        scratch_shapes=[pltpu.VMEM((2 * NB, PW), BF16), pltpu.VMEM((2 * NB, PW), BF16)],
        name="row_side",
    )(place, readers.reshape(-1), row_own, row_other, partner, diag, side)

    out = pl.pallas_call(
        update_kernel,
        grid=(4,),
        out_shape=jax.ShapeDtypeStruct((8, 8 * NB, NB), F32),
        in_specs=[
            smem(),
            smem(),
            smem(),
            pl.BlockSpec((2, 8 * NB, NB), lambda s: (s, 0, 0)),
            pl.BlockSpec((2, 4, 3, NB, NB), lambda s: (s, 0, 0, 0, 0)),
            vmem(),
            by_two,
            by_two,
            vmem(),
            vmem(),
            vmem(),
            vmem(),
            vmem(),
        ],
        out_specs=pl.BlockSpec((2, 8 * NB, NB), lambda s: (s, 0, 0)),
        scratch_shapes=[pltpu.VMEM((8 * NB, PW), BF16), pltpu.VMEM((8 * NB, PW), BF16)],
        name="update",
    )(place, adj, readers.reshape(-1), front, own, faces_x, w0r, w1r, cross, col_half, partner, diag, side)
    return out.reshape(8, 1, NB, 8, 1, NB)


def solution(mesh):
    in_specs = (
        P(None, "row", None, None, "col", None),
        P(None, "row", None, None, None, None),
        P(),
        P(),
        P(),
        P(),
        P(),
        P(),
    )
    out_specs = P(None, "row", None, None, "col", None)
    return jax.shard_map(steps, mesh=mesh, in_specs=in_specs, out_specs=out_specs, check_vma=False)
```

```python
import jax
import jax.numpy as jnp
from jax import lax
from jax.experimental import pallas as pl
from jax.experimental.pallas import tpu as pltpu
from jax.sharding import PartitionSpec as P


NB = 128
PW = 512
N = 16
BOTH = ("row", "col")
F32 = jnp.float32
BF16 = jnp.bfloat16

SWAP_X = [(r, r ^ 1) for r in range(N)]
Z_LINES = [[2 * z + x for z in range(8)] for x in (0, 1)]


def spread_target(q, j):
    return 2 * ((q // 2 + j // 2) % 8) + j % 2


SPREAD = [(q * N + j, spread_target(q, j) * N + q) for q in range(N) for j in range(N)]
LOW_A = [(s, d) for s, d in SPREAD if s // N < 8]
LOW_B = [(s, d + 8) for s, d in LOW_A]
HALVE = [(n, n + 8) for n in range(8)]
SWAP_CORE = [(c, c ^ 1) for c in range(N)]
SAME_CORE = [[2 * i + k for i in range(8)] for k in (0, 1)]


def left_of(ref, lead):
    v, s, l = ref[lead + (0,)], ref[lead + (1,)], ref[lead + (2,)]
    return jnp.concatenate([v, v, s, l], axis=0)


def right_of_parts(v, s, l):
    return jnp.concatenate([v * 4.0, s * -0.5, v * -0.5, l * 2.0], axis=0).astype(BF16)


def right_of(ref, lead):
    return right_of_parts(ref[lead + (0,)], ref[lead + (1,)], ref[lead + (2,)])


def right_of_chunks(chunks):
    rows = jnp.concatenate(chunks, axis=0)
    return right_of_parts(rows[:NB], rows[NB : 2 * NB], rows[2 * NB :])


def pair_product(left, right):
    return lax.dot_general(left, right, (((0,), (0,)), ((), ())), preferred_element_type=F32)


def panel_block_kernel(place, adj, base, own, faces, half, first, acc):
    r, c = place[0], place[1]
    n = c % 8
    acc[...] = base[...]

    def add(a, value):
        t = a - 4 * (c // 8)

        @pl.when((t >= 0) & (t < 4))
        def _():
            acc[jnp.clip(t, 0, 3)] += value

        @pl.when(a == 0)
        def _():
            acc[4] += value

    for g in range(4):
        e = adj[n * 4 + g]

        @pl.when(e % N == r)
        def _():
            right = right_of_chunks([faces[2 * (4 * (g % 2) + k) + g // 2] for k in range(4)])
            add(e // N, -pair_product(left_of(own, (e // N, g ^ 1)), right))

    @pl.when(r == n)
    def _():
        for f in range(4):
            add(jnp.int32(0), pair_product(left_of(own, (0, f)), right_of(own, (0, f))))

    half[...] = acc[:4].astype(BF16)
    first[...] = acc[4:].astype(BF16)


def couple_kernel(place, adj, own, faces, out):
    r, c = place[0], place[1]

    def one_class(q, carry):
        for h in range(2):
            e = adj[((c // 2) * N + q) * 4 + 2 * (c % 2) + h]

            @pl.when(e % N == r)
            def _():
                right = right_of(faces, (q // 2, (q % 2) ^ (r % 2), h))
                out[q, h] = pair_product(left_of(own, (e // N, 2 * (c % 2) + 1 - h)), right).astype(BF16)

        return carry

    lax.fori_loop(0, N, one_class, 0)


def assemble_kernel(place, base, own, out):
    r, c = place[0], place[1]
    out[...] = base[...]

    @pl.when(r == c)
    def _():
        total = pair_product(left_of(own, (0, 0)), right_of(own, (0, 0)))
        for f in range(1, 4):
            total += pair_product(left_of(own, (0, f)), right_of(own, (0, f)))
        rows = pl.ds(pl.program_id(0), NB, stride=8)
        out[0, rows, :] = out[0, rows, :] + total


def dot_nt(x, y):
    return lax.dot_general(x, y, (((1,), (1,)), ((), ())), preferred_element_type=F32)


def scale(values, partner, diag, side):
    swapped = jnp.dot(values, partner, preferred_element_type=F32)
    return (values.astype(F32) * diag + swapped * side).astype(BF16)


def keep(readers, k, e):
    return jnp.where((readers[k * 128 + e] == 1) & (e >= 4 * (k + 1)), 1.0, 0.0).astype(F32)


def row_side_kernel(place, readers, row_own, row_other, partner, diag, side, w0r, w1r, cross, v0r, f1r):
    r, c = place[0], place[1]
    step = pl.program_id(0)

    def tile_of(n, chunk, slot):
        at = (n // 2 + 4 * chunk, slot)
        return jnp.where(c % 2 == n % 2, row_own[at], row_other[at])

    @pl.when(step == 0)
    def _():
        for i in range(4):
            kept = keep(readers, 0, 4 + i)
            for n in range(4):
                tile = tile_of(n, i // 2, 4 + i % 2).astype(F32) * kept
                cross[i * NB : (i + 1) * NB, n * NB : (n + 1) * NB] = tile.astype(BF16)

    for t in range(2):
        a = 2 * step + t
        kept = keep(readers, 0, a * N + r)
        rows = slice(t * NB, (t + 1) * NB)
        for n in range(8):
            tile = tile_of(n, a // 4, a % 4)
            if n < 4:
                v0r[rows, n * NB : (n + 1) * NB] = (tile.astype(F32) * kept).astype(BF16)
            else:
                f1r[rows, (n - 4) * NB : (n - 3) * NB] = tile
    w0 = scale(v0r[...], partner[0], diag[0:1], side[0:1])
    w0r[...] = w0
    fresh = f1r[...].astype(F32) - dot_nt(w0, cross[...])
    for t in range(2):
        kept = keep(readers, 1, (2 * step + t) * N + r)
        f1r[t * NB : (t + 1) * NB, :] = (fresh[t * NB : (t + 1) * NB] * kept).astype(BF16)
    w1r[...] = scale(f1r[...], partner[1], diag[1:2], side[1:2])


def update_kernel(
    place, adj, readers, front, couplings, w0r, w1r, cross, col_half, partner, diag, side, out, v0c, v1c,
):
    r, c = place[0], place[1]
    step = pl.program_id(0)

    @pl.when(step == 0)
    def _():
        for b in range(8):
            kept = keep(readers, 0, b * N + c)
            for n in range(8):
                j = n + 8 * (b // 4)
                tile = col_half[(j // 2 + c // 2) % 8, (j % 2) ^ (r % 2), b % 4]
                rows = slice(b * NB, (b + 1) * NB)
                if n < 4:
                    v0c[rows, n * NB : (n + 1) * NB] = (tile.astype(F32) * kept).astype(BF16)
                else:
                    v1c[rows, (n - 4) * NB : (n - 3) * NB] = tile
        w0c = scale(v0c[...], partner[0], diag[0:1], side[0:1])
        fresh = v1c[...].astype(F32) - dot_nt(w0c, cross[...])
        for b in range(8):
            kept = keep(readers, 1, b * N + c)
            v1c[b * NB : (b + 1) * NB, :] = (fresh[b * NB : (b + 1) * NB] * kept).astype(BF16)

    change = dot_nt(w0r[...], v0c[...]) + dot_nt(w1r[...], v1c[...])
    for t in range(2):
        for b in range(8):
            rows = pl.ds(b, NB, stride=8)
            out[t, rows, :] = front[t, rows, :] - change[t * NB : (t + 1) * NB, b * NB : (b + 1) * NB]
        for f in range(4):
            n = adj[((2 * step + t) * N + r) * 4 + f]

            @pl.when(n % N == c)
            def _():
                g = f ^ 1
                rows = pl.ds(n // N, NB, stride=8)
                out[t, rows, :] = out[t, rows, :] - couplings[2 * (n // N) + g // 2, g % 2].astype(F32)


def pivot_tables(pivot_order, pivot_kind, inverse_diagonal, inverse_coupling):
    at = pivot_order[:, :, None] == jnp.arange(PW, dtype=jnp.int32)[None, None, :]
    starts = jnp.where(pivot_kind == 1, inverse_coupling, 0.0).reshape(2, PW // 2, 2)[:, :, 0]
    factor = jnp.repeat(starts, 2, axis=1)
    diag = jnp.sum(jnp.where(at, inverse_diagonal[:, :, None], 0.0), axis=1)
    side = jnp.sum(jnp.where(at, factor[:, :, None], 0.0), axis=1)
    order_swapped = pivot_order.reshape(2, PW // 2, 2)[:, :, ::-1].reshape(2, PW)
    partner_of = jnp.sum(jnp.where(at, order_swapped[:, :, None], 0), axis=1)
    partner = (jnp.arange(PW, dtype=jnp.int32)[None, :, None] == partner_of[:, None, :]).astype(BF16)
    return partner, diag, side


def smem():
    return pl.BlockSpec(memory_space=pltpu.SMEM)


def vmem():
    return pl.BlockSpec(memory_space=pltpu.VMEM)


def steps(
    front_base, traces, adjacency, pivot_order, pivot_kind, inverse_diagonal, inverse_coupling, readers,
):
    r = lax.axis_index("row")
    c = lax.axis_index("col")
    place = jnp.stack([r, c]).astype(jnp.int32)
    adj = adjacency.reshape(-1)
    own = traces[:, 0]
    base = front_base.reshape(8, 8 * NB, NB)

    mine = lax.dynamic_slice_in_dim(own.reshape(32, 3, NB, NB), 2 * c, 2, axis=0)
    mine_x = lax.ppermute(mine, "row", SWAP_X)
    faces = lax.all_gather(jnp.stack([mine, mine_x]), "row", axis=0, axis_index_groups=Z_LINES)

    chunk = (r // 2 + c // 2) % 8 + 8 * (c % 2)
    low = lax.dynamic_index_in_dim(own[0].reshape(N, 96, NB), chunk, 0, keepdims=False)
    low_a = lax.ppermute(low, BOTH, LOW_A)
    low_b = lax.ppermute(low, BOTH, LOW_B)
    low = jnp.where(c < 8, low_a, low_b)
    low_faces = lax.all_to_all(jnp.broadcast_to(low[None], (N, 96, NB)), "row", 0, 0, tiled=True)

    base_low = front_base[:, 0, :, 0, 0, :]
    base_far = lax.ppermute(jnp.concatenate([base_low[4:], base_low[:1]]), "col", HALVE)
    half, first = pl.pallas_call(
        panel_block_kernel,
        out_shape=(jax.ShapeDtypeStruct((4, NB, NB), BF16), jax.ShapeDtypeStruct((1, NB, NB), BF16)),
        in_specs=[smem(), smem(), vmem(), vmem(), vmem()],
        out_specs=(vmem(), vmem()),
        scratch_shapes=[pltpu.VMEM((5, NB, NB), F32)],
        name="panel_block",
    )(place, adj, jnp.where(c < 8, jnp.concatenate([base_low[:4], base_low[:1]]), base_far), own, low_faces)

    spread = lax.ppermute(half, BOTH, SPREAD)
    other = lax.ppermute(spread, "row", SWAP_X)
    pair, faces = lax.optimization_barrier((jnp.stack([spread, other]), faces))
    col_half = lax.all_gather(pair, "row", axis=0, axis_index_groups=Z_LINES)

    cross_row = lax.all_to_all(jnp.broadcast_to(first, (N, NB, NB)), "row", 0, 0, tiled=True)[4:8]

    half = jnp.concatenate([half, jnp.where(c < 8, cross_row[:2], cross_row[2:])])
    row_own = lax.all_to_all(
        jnp.broadcast_to(half[None], (8,) + half.shape), "col", 0, 0, tiled=True, axis_index_groups=SAME_CORE
    )
    row_other = lax.ppermute(row_own, "col", SWAP_CORE)

    partner, diag, side = pivot_tables(pivot_order, pivot_kind, inverse_diagonal, inverse_coupling)

    couplings = pl.pallas_call(
        couple_kernel,
        out_shape=jax.ShapeDtypeStruct((N, 2, NB, NB), BF16),
        in_specs=[smem(), smem(), vmem(), vmem()],
        out_specs=vmem(),
        name="couple",
    )(place, adj, own, faces)
    couplings = lax.all_to_all(couplings, "col", 0, 0, tiled=True)

    front = pl.pallas_call(
        assemble_kernel,
        grid=(8,),
        out_shape=jax.ShapeDtypeStruct((8, 8 * NB, NB), F32),
        in_specs=[
            smem(),
            pl.BlockSpec((1, 8 * NB, NB), lambda a: (a, 0, 0)),
            pl.BlockSpec((1, 4, 3, NB, NB), lambda a: (a, 0, 0, 0, 0)),
        ],
        out_specs=pl.BlockSpec((1, 8 * NB, NB), lambda a: (a, 0, 0)),
        name="assemble",
    )(place, base, own)

    by_two = pl.BlockSpec((2 * NB, PW), lambda s: (s, 0))
    w0r, w1r, cross = pl.pallas_call(
        row_side_kernel,
        grid=(4,),
        out_shape=(jax.ShapeDtypeStruct((8 * NB, PW), BF16),) * 2 + (jax.ShapeDtypeStruct((PW, PW), BF16),),
        in_specs=[smem(), smem(), vmem(), vmem(), vmem(), vmem(), vmem()],
        out_specs=(by_two, by_two, pl.BlockSpec((PW, PW), lambda s: (0, 0))),
        scratch_shapes=[pltpu.VMEM((2 * NB, PW), BF16), pltpu.VMEM((2 * NB, PW), BF16)],
        name="row_side",
    )(place, readers.reshape(-1), row_own, row_other, partner, diag, side)

    out = pl.pallas_call(
        update_kernel,
        grid=(4,),
        out_shape=jax.ShapeDtypeStruct((8, 8 * NB, NB), F32),
        in_specs=[
            smem(),
            smem(),
            smem(),
            pl.BlockSpec((2, 8 * NB, NB), lambda s: (s, 0, 0)),
            vmem(),
            by_two,
            by_two,
            vmem(),
            vmem(),
            vmem(),
            vmem(),
            vmem(),
        ],
        out_specs=pl.BlockSpec((2, 8 * NB, NB), lambda s: (s, 0, 0)),
        scratch_shapes=[pltpu.VMEM((8 * NB, PW), BF16), pltpu.VMEM((8 * NB, PW), BF16)],
        name="update",
    )(place, adj, readers.reshape(-1), front, couplings, w0r, w1r, cross, col_half, partner, diag, side)
    return out.reshape(8, 1, NB, 8, 1, NB)


def solution(mesh):
    in_specs = (
        P(None, "row", None, None, "col", None),
        P(None, "row", None, None, None, None),
        P(),
        P(),
        P(),
        P(),
        P(),
        P(),
    )
    out_specs = P(None, "row", None, None, "col", None)
    return jax.shard_map(steps, mesh=mesh, in_specs=in_specs, out_specs=out_specs, check_vma=False)
```

```python
import jax
import jax.numpy as jnp
from jax import lax
from jax.experimental import pallas as pl
from jax.experimental.pallas import tpu as pltpu
from jax.sharding import PartitionSpec as P


NB = 128
PW = 512
N = 16
BOTH = ("row", "col")
F32 = jnp.float32
BF16 = jnp.bfloat16

SWAP_X = [(r, r ^ 1) for r in range(N)]
Z_LINES = [[2 * z + x for z in range(8)] for x in (0, 1)]


def spread_target(q, j):
    return 2 * ((q // 2 + j // 2) % 8) + j % 2


SPREAD = [(q * N + j, spread_target(q, j) * N + q) for q in range(N) for j in range(N)]
LOW_A = [(s, d) for s, d in SPREAD if s // N < 8]
LOW_B = [(s, d + 8) for s, d in LOW_A]
HALVE = [(n, n + 8) for n in range(8)]
SWAP_CORE = [(c, c ^ 1) for c in range(N)]
SAME_CORE = [[2 * i + k for i in range(8)] for k in (0, 1)]


def left_of(ref, lead):
    v, s, l = ref[lead + (0,)], ref[lead + (1,)], ref[lead + (2,)]
    return jnp.concatenate([v, v, s, l], axis=0)


def right_of_parts(v, s, l):
    return jnp.concatenate([v * 4.0, s * -0.5, v * -0.5, l * 2.0], axis=0).astype(BF16)


def right_of(ref, lead):
    return right_of_parts(ref[lead + (0,)], ref[lead + (1,)], ref[lead + (2,)])


def right_of_chunks(chunks):
    rows = jnp.concatenate(chunks, axis=0)
    return right_of_parts(rows[:NB], rows[NB : 2 * NB], rows[2 * NB :])


def pair_product(left, right):
    return lax.dot_general(left, right, (((0,), (0,)), ((), ())), preferred_element_type=F32)


def panel_block_kernel(place, adj, base, own, faces, half, first, acc):
    r, c = place[0], place[1]
    n = c % 8
    acc[...] = base[...]

    def add(a, value):
        t = a - 4 * (c // 8)

        @pl.when((t >= 0) & (t < 4))
        def _():
            acc[jnp.clip(t, 0, 3)] += value

        @pl.when(a == 0)
        def _():
            acc[4] += value

    for g in range(4):
        e = adj[n * 4 + g]

        @pl.when(e % N == r)
        def _():
            right = right_of_chunks([faces[2 * (4 * (g % 2) + k) + g // 2] for k in range(4)])
            add(e // N, -pair_product(left_of(own, (e // N, g ^ 1)), right))

    @pl.when(r == n)
    def _():
        for f in range(4):
            add(jnp.int32(0), pair_product(left_of(own, (0, f)), right_of(own, (0, f))))

    half[...] = acc[:4].astype(BF16)
    first[0] = acc[4, pl.ds(pl.multiple_of((NB // 2) * (c // 8), NB // 2), NB // 2), :].astype(BF16)


def couple_kernel(place, adj, own, faces, out):
    r, c = place[0], place[1]

    def one_class(q, carry):
        for h in range(2):
            e = adj[((c // 2) * N + q) * 4 + 2 * (c % 2) + h]

            @pl.when(e % N == r)
            def _():
                right = right_of(faces, (q // 2, (q % 2) ^ (r % 2), h))
                out[q, h] = pair_product(left_of(own, (e // N, 2 * (c % 2) + 1 - h)), right).astype(BF16)

        return carry

    lax.fori_loop(0, N, one_class, 0)


def assemble_kernel(place, base, own, out):
    r, c = place[0], place[1]
    out[...] = base[...]

    @pl.when(r == c)
    def _():
        total = pair_product(left_of(own, (0, 0)), right_of(own, (0, 0)))
        for f in range(1, 4):
            total += pair_product(left_of(own, (0, f)), right_of(own, (0, f)))
        rows = pl.ds(pl.program_id(0), NB, stride=8)
        out[0, rows, :] = out[0, rows, :] + total


def dot_nt(x, y):
    return lax.dot_general(x, y, (((1,), (1,)), ((), ())), preferred_element_type=F32)


def scale(values, partner, diag, side):
    swapped = jnp.dot(values, partner, preferred_element_type=F32)
    return (values.astype(F32) * diag + swapped * side).astype(BF16)


def keep(readers, k, e):
    return jnp.where((readers[k * 128 + e] == 1) & (e >= 4 * (k + 1)), 1.0, 0.0).astype(F32)


def row_side_kernel(place, readers, row_own, row_other, partner, diag, side, w0r, w1r, cross, v0r, f1r):
    r, c = place[0], place[1]
    step = pl.program_id(0)

    def tile_of(n, chunk, slot):
        at = (n // 2 + 4 * chunk, slot)
        return jnp.where(c % 2 == n % 2, row_own[at], row_other[at])

    @pl.when(step == 0)
    def _():
        for i in range(4):
            kept = keep(readers, 0, 4 + i)
            for n in range(4):
                for h in range(2):
                    tile = tile_of(n, h, 4 + i // 2)[(i % 2) * (NB // 2) : (i % 2 + 1) * (NB // 2)].astype(F32) * kept
                    top = i * NB + h * (NB // 2)
                    cross[top : top + NB // 2, n * NB : (n + 1) * NB] = tile.astype(BF16)

    for t in range(2):
        a = 2 * step + t
        kept = keep(readers, 0, a * N + r)
        rows = slice(t * NB, (t + 1) * NB)
        for n in range(8):
            tile = tile_of(n, a // 4, a % 4)
            if n < 4:
                v0r[rows, n * NB : (n + 1) * NB] = (tile.astype(F32) * kept).astype(BF16)
            else:
                f1r[rows, (n - 4) * NB : (n - 3) * NB] = tile
    w0 = scale(v0r[...], partner[0], diag[0:1], side[0:1])
    w0r[...] = w0
    fresh = f1r[...].astype(F32) - dot_nt(w0, cross[...])
    for t in range(2):
        kept = keep(readers, 1, (2 * step + t) * N + r)
        f1r[t * NB : (t + 1) * NB, :] = (fresh[t * NB : (t + 1) * NB] * kept).astype(BF16)
    w1r[...] = scale(f1r[...], partner[1], diag[1:2], side[1:2])


def update_kernel(
    place, adj, readers, front, couplings, w0r, w1r, cross, col_half, partner, diag, side, out, v0c, v1c,
):
    r, c = place[0], place[1]
    step = pl.program_id(0)

    @pl.when(step == 0)
    def _():
        for b in range(8):
            kept = keep(readers, 0, b * N + c)
            for n in range(8):
                j = n + 8 * (b // 4)
                tile = col_half[(j // 2 + c // 2) % 8, (j % 2) ^ (r % 2), b % 4]
                rows = slice(b * NB, (b + 1) * NB)
                if n < 4:
                    v0c[rows, n * NB : (n + 1) * NB] = (tile.astype(F32) * kept).astype(BF16)
                else:
                    v1c[rows, (n - 4) * NB : (n - 3) * NB] = tile
        w0c = scale(v0c[...], partner[0], diag[0:1], side[0:1])
        fresh = v1c[...].astype(F32) - dot_nt(w0c, cross[...])
        for b in range(8):
            kept = keep(readers, 1, b * N + c)
            v1c[b * NB : (b + 1) * NB, :] = (fresh[b * NB : (b + 1) * NB] * kept).astype(BF16)

    change = dot_nt(w0r[...], v0c[...]) + dot_nt(w1r[...], v1c[...])
    for t in range(4):
        for b in range(8):
            rows = pl.ds(b, NB, stride=8)
            out[t, rows, :] = front[t, rows, :] - change[t * NB : (t + 1) * NB, b * NB : (b + 1) * NB]
        for f in range(4):
            n = adj[((4 * step + t) * N + r) * 4 + f]

            @pl.when(n % N == c)
            def _():
                g = f ^ 1
                rows = pl.ds(n // N, NB, stride=8)
                out[t, rows, :] = out[t, rows, :] - couplings[2 * (n // N) + g // 2, g % 2].astype(F32)


def pivot_tables(pivot_order, pivot_kind, inverse_diagonal, inverse_coupling):
    at = pivot_order[:, :, None] == jnp.arange(PW, dtype=jnp.int32)[None, None, :]
    starts = jnp.where(pivot_kind == 1, inverse_coupling, 0.0).reshape(2, PW // 2, 2)[:, :, 0]
    factor = jnp.repeat(starts, 2, axis=1)
    diag = jnp.sum(jnp.where(at, inverse_diagonal[:, :, None], 0.0), axis=1)
    side = jnp.sum(jnp.where(at, factor[:, :, None], 0.0), axis=1)
    order_swapped = pivot_order.reshape(2, PW // 2, 2)[:, :, ::-1].reshape(2, PW)
    partner_of = jnp.sum(jnp.where(at, order_swapped[:, :, None], 0), axis=1)
    partner = (jnp.arange(PW, dtype=jnp.int32)[None, :, None] == partner_of[:, None, :]).astype(BF16)
    return partner, diag, side


def smem():
    return pl.BlockSpec(memory_space=pltpu.SMEM)


def vmem():
    return pl.BlockSpec(memory_space=pltpu.VMEM)


def steps(
    front_base, traces, adjacency, pivot_order, pivot_kind, inverse_diagonal, inverse_coupling, readers,
):
    r = lax.axis_index("row")
    c = lax.axis_index("col")
    place = jnp.stack([r, c]).astype(jnp.int32)
    adj = adjacency.reshape(-1)
    own = traces[:, 0]
    base = front_base.reshape(8, 8 * NB, NB)

    mine = lax.dynamic_slice_in_dim(own.reshape(32, 3, NB, NB), 2 * c, 2, axis=0)
    mine_x = lax.ppermute(mine, "row", SWAP_X)
    faces = lax.all_gather(jnp.stack([mine, mine_x]), "row", axis=0, axis_index_groups=Z_LINES)

    chunk = (r // 2 + c // 2) % 8 + 8 * (c % 2)
    low = lax.dynamic_index_in_dim(own[0].reshape(N, 96, NB), chunk, 0, keepdims=False)
    low_a = lax.ppermute(low, BOTH, LOW_A)
    low_b = lax.ppermute(low, BOTH, LOW_B)
    low = jnp.where(c < 8, low_a, low_b)
    low_faces = lax.all_to_all(jnp.broadcast_to(low[None], (N, 96, NB)), "row", 0, 0, tiled=True)

    base_low = front_base[:, 0, :, 0, 0, :]
    base_far = lax.ppermute(jnp.concatenate([base_low[4:], base_low[:1]]), "col", HALVE)
    half, first = pl.pallas_call(
        panel_block_kernel,
        out_shape=(jax.ShapeDtypeStruct((4, NB, NB), BF16), jax.ShapeDtypeStruct((1, NB // 2, NB), BF16)),
        in_specs=[smem(), smem(), vmem(), vmem(), vmem()],
        out_specs=(vmem(), vmem()),
        scratch_shapes=[pltpu.VMEM((5, NB, NB), F32)],
        name="panel_block",
    )(place, adj, jnp.where(c < 8, jnp.concatenate([base_low[:4], base_low[:1]]), base_far), own, low_faces)

    spread = lax.ppermute(half, BOTH, SPREAD)
    other = lax.ppermute(spread, "row", SWAP_X)
    pair = jnp.stack([spread, other])
    col_half = lax.all_gather(pair, "row", axis=0, axis_index_groups=Z_LINES)

    cross_row = lax.all_to_all(jnp.broadcast_to(first, (N, NB // 2, NB)), "row", 0, 0, tiled=True)[4:8]

    half = jnp.concatenate([half, cross_row.reshape(2, NB, NB)])
    row_own = lax.all_to_all(
        jnp.broadcast_to(half[None], (8,) + half.shape), "col", 0, 0, tiled=True, axis_index_groups=SAME_CORE
    )
    row_other = lax.ppermute(row_own, "col", SWAP_CORE)

    partner, diag, side = pivot_tables(pivot_order, pivot_kind, inverse_diagonal, inverse_coupling)

    couplings = pl.pallas_call(
        couple_kernel,
        out_shape=jax.ShapeDtypeStruct((N, 2, NB, NB), BF16),
        in_specs=[smem(), smem(), vmem(), vmem()],
        out_specs=vmem(),
        name="couple",
    )(place, adj, own, faces)
    couplings = lax.all_to_all(couplings, "col", 0, 0, tiled=True)

    front = pl.pallas_call(
        assemble_kernel,
        grid=(8,),
        out_shape=jax.ShapeDtypeStruct((8, 8 * NB, NB), F32),
        in_specs=[
            smem(),
            pl.BlockSpec((1, 8 * NB, NB), lambda a: (a, 0, 0)),
            pl.BlockSpec((1, 4, 3, NB, NB), lambda a: (a, 0, 0, 0, 0)),
        ],
        out_specs=pl.BlockSpec((1, 8 * NB, NB), lambda a: (a, 0, 0)),
        name="assemble",
    )(place, base, own)

    by_two = pl.BlockSpec((2 * NB, PW), lambda s: (s, 0))
    w0r, w1r, cross = pl.pallas_call(
        row_side_kernel,
        grid=(4,),
        out_shape=(jax.ShapeDtypeStruct((8 * NB, PW), BF16),) * 2 + (jax.ShapeDtypeStruct((PW, PW), BF16),),
        in_specs=[smem(), smem(), vmem(), vmem(), vmem(), vmem(), vmem()],
        out_specs=(by_two, by_two, pl.BlockSpec((PW, PW), lambda s: (0, 0))),
        scratch_shapes=[pltpu.VMEM((2 * NB, PW), BF16), pltpu.VMEM((2 * NB, PW), BF16)],
        name="row_side",
    )(place, readers.reshape(-1), row_own, row_other, partner, diag, side)

    out = pl.pallas_call(
        update_kernel,
        grid=(2,),
        out_shape=jax.ShapeDtypeStruct((8, 8 * NB, NB), F32),
        in_specs=[
            smem(),
            smem(),
            smem(),
            pl.BlockSpec((4, 8 * NB, NB), lambda s: (s, 0, 0)),
            vmem(),
            pl.BlockSpec((4 * NB, PW), lambda s: (s, 0)),
            pl.BlockSpec((4 * NB, PW), lambda s: (s, 0)),
            vmem(),
            vmem(),
            vmem(),
            vmem(),
            vmem(),
        ],
        out_specs=pl.BlockSpec((4, 8 * NB, NB), lambda s: (s, 0, 0)),
        scratch_shapes=[pltpu.VMEM((8 * NB, PW), BF16), pltpu.VMEM((8 * NB, PW), BF16)],
        name="update",
    )(place, adj, readers.reshape(-1), front, couplings, w0r, w1r, cross, col_half, partner, diag, side)
    return out.reshape(8, 1, NB, 8, 1, NB)


def solution(mesh):
    in_specs = (
        P(None, "row", None, None, "col", None),
        P(None, "row", None, None, None, None),
        P(),
        P(),
        P(),
        P(),
        P(),
        P(),
    )
    out_specs = P(None, "row", None, None, "col", None)
    return jax.shard_map(steps, mesh=mesh, in_specs=in_specs, out_specs=out_specs, check_vma=False)
```

```python
import jax
import jax.numpy as jnp
from jax import lax
from jax.experimental import pallas as pl
from jax.experimental.pallas import tpu as pltpu
from jax.sharding import PartitionSpec as P


NB = 128
PW = 512
N = 16
BOTH = ("row", "col")
F32 = jnp.float32
BF16 = jnp.bfloat16

SWAP_X = [(r, r ^ 1) for r in range(N)]
Z_LINES = [[2 * z + x for z in range(8)] for x in (0, 1)]


def spread_target(q, j):
    return 2 * ((q // 2 + j // 2) % 8) + j % 2


SPREAD = [(q * N + j, spread_target(q, j) * N + q) for q in range(N) for j in range(N)]
LOW_A = [(s, d) for s, d in SPREAD if s // N < 8]
LOW_B = [(s, d + 8) for s, d in LOW_A]
HALVE = [(n, n + 8) for n in range(8)]
SWAP_CORE = [(c, c ^ 1) for c in range(N)]
SAME_CORE = [[2 * i + k for i in range(8)] for k in (0, 1)]


def left_of(ref, lead):
    v, s, l = ref[lead + (0,)], ref[lead + (1,)], ref[lead + (2,)]
    return jnp.concatenate([v, v, s, l], axis=0)


def right_of_parts(v, s, l):
    return jnp.concatenate([v * 4.0, s * -0.5, v * -0.5, l * 2.0], axis=0).astype(BF16)


def right_of(ref, lead):
    return right_of_parts(ref[lead + (0,)], ref[lead + (1,)], ref[lead + (2,)])


def right_of_chunks(chunks):
    rows = jnp.concatenate(chunks, axis=0)
    return right_of_parts(rows[:NB], rows[NB : 2 * NB], rows[2 * NB :])


def pair_product(left, right):
    return lax.dot_general(left, right, (((0,), (0,)), ((), ())), preferred_element_type=F32)


def panel_block_kernel(place, adj, base, own, faces, half, first, acc):
    r, c = place[0], place[1]
    n = c % 8
    acc[...] = base[...]

    def add(a, value):
        t = a - 4 * (c // 8)

        @pl.when((t >= 0) & (t < 4))
        def _():
            acc[jnp.clip(t, 0, 3)] += value

        @pl.when(a == 0)
        def _():
            acc[4] += value

    for g in range(4):
        e = adj[n * 4 + g]

        @pl.when(e % N == r)
        def _():
            right = right_of_chunks([faces[2 * (4 * (g % 2) + k) + g // 2] for k in range(4)])
            add(e // N, -pair_product(left_of(own, (e // N, g ^ 1)), right))

    @pl.when(r == n)
    def _():
        for f in range(4):
            add(jnp.int32(0), pair_product(left_of(own, (0, f)), right_of(own, (0, f))))

    half[...] = acc[:4].astype(BF16)
    first[0] = acc[4, pl.ds(pl.multiple_of((NB // 2) * (c // 8), NB // 2), NB // 2), :].astype(BF16)


def couple_kernel(place, adj, own, faces, out):
    r, c = place[0], place[1]

    def one_class(q, carry):
        for h in range(2):
            e = adj[((c // 2) * N + q) * 4 + 2 * (c % 2) + h]

            @pl.when(e % N == r)
            def _():
                right = right_of(faces, (q // 2, (q % 2) ^ (r % 2), h))
                out[q, h] = pair_product(left_of(own, (e // N, 2 * (c % 2) + 1 - h)), right).astype(BF16)

        return carry

    lax.fori_loop(0, N, one_class, 0)


def assemble_kernel(place, base, own, out):
    r, c = place[0], place[1]
    out[...] = base[...]

    @pl.when(r == c)
    def _():
        total = pair_product(left_of(own, (0, 0)), right_of(own, (0, 0)))
        for f in range(1, 4):
            total += pair_product(left_of(own, (0, f)), right_of(own, (0, f)))
        rows = pl.ds(pl.program_id(0), NB, stride=8)
        out[0, rows, :] = out[0, rows, :] + total


def dot_nt(x, y):
    return lax.dot_general(x, y, (((1,), (1,)), ((), ())), preferred_element_type=F32)


def scale(values, partner, diag, side):
    swapped = jnp.dot(values, partner, preferred_element_type=F32)
    return (values.astype(F32) * diag + swapped * side).astype(BF16)


def keep(readers, k, e):
    return jnp.where((readers[k * 128 + e] == 1) & (e >= 4 * (k + 1)), 1.0, 0.0).astype(F32)


def row_side_kernel(place, readers, row_own, row_other, partner, diag, side, w0r, w1r, cross, v0r, f1r):
    r, c = place[0], place[1]
    step = pl.program_id(0)

    def tile_of(n, chunk, slot):
        at = (n // 2 + 4 * chunk, slot)
        return jnp.where(c % 2 == n % 2, row_own[at], row_other[at])

    @pl.when(step == 0)
    def _():
        for i in range(4):
            kept = keep(readers, 0, 4 + i)
            for n in range(4):
                for h in range(2):
                    tile = tile_of(n, h, 4 + i // 2)[(i % 2) * (NB // 2) : (i % 2 + 1) * (NB // 2)].astype(F32) * kept
                    top = i * NB + h * (NB // 2)
                    cross[top : top + NB // 2, n * NB : (n + 1) * NB] = tile.astype(BF16)

    for t in range(2):
        a = 2 * step + t
        kept = keep(readers, 0, a * N + r)
        rows = slice(t * NB, (t + 1) * NB)
        for n in range(8):
            tile = tile_of(n, a // 4, a % 4)
            if n < 4:
                v0r[rows, n * NB : (n + 1) * NB] = (tile.astype(F32) * kept).astype(BF16)
            else:
                f1r[rows, (n - 4) * NB : (n - 3) * NB] = tile
    w0 = scale(v0r[...], partner[0], diag[0:1], side[0:1])
    w0r[...] = w0
    fresh = f1r[...].astype(F32) - dot_nt(w0, cross[...])
    for t in range(2):
        kept = keep(readers, 1, (2 * step + t) * N + r)
        f1r[t * NB : (t + 1) * NB, :] = (fresh[t * NB : (t + 1) * NB] * kept).astype(BF16)
    w1r[...] = scale(f1r[...], partner[1], diag[1:2], side[1:2])


def update_kernel(
    place, adj, readers, front, couplings, w0r, w1r, cross, col_half, partner, diag, side, out, v0c, v1c,
):
    r, c = place[0], place[1]
    step = pl.program_id(0)

    @pl.when(step == 0)
    def _():
        for b in range(8):
            kept = keep(readers, 0, b * N + c)
            for n in range(8):
                j = n + 8 * (b // 4)
                tile = col_half[(j // 2 + c // 2) % 8, (j % 2) ^ (r % 2), b % 4]
                rows = slice(b * NB, (b + 1) * NB)
                if n < 4:
                    v0c[rows, n * NB : (n + 1) * NB] = (tile.astype(F32) * kept).astype(BF16)
                else:
                    v1c[rows, (n - 4) * NB : (n - 3) * NB] = tile
        w0c = scale(v0c[...], partner[0], diag[0:1], side[0:1])
        fresh = v1c[...].astype(F32) - dot_nt(w0c, cross[...])
        for b in range(8):
            kept = keep(readers, 1, b * N + c)
            v1c[b * NB : (b + 1) * NB, :] = (fresh[b * NB : (b + 1) * NB] * kept).astype(BF16)

    change = dot_nt(w0r[...], v0c[...]) + dot_nt(w1r[...], v1c[...])
    for t in range(4):
        for b in range(8):
            rows = pl.ds(b, NB, stride=8)
            out[t, rows, :] = front[t, rows, :] - change[t * NB : (t + 1) * NB, b * NB : (b + 1) * NB]
        for f in range(4):
            n = adj[((4 * step + t) * N + r) * 4 + f]

            @pl.when(n % N == c)
            def _():
                g = f ^ 1
                rows = pl.ds(n // N, NB, stride=8)
                out[t, rows, :] = out[t, rows, :] - couplings[2 * (n // N) + g // 2, g % 2].astype(F32)


def pivot_tables(pivot_order, pivot_kind, inverse_diagonal, inverse_coupling):
    at = pivot_order[:, :, None] == jnp.arange(PW, dtype=jnp.int32)[None, None, :]
    starts = jnp.where(pivot_kind == 1, inverse_coupling, 0.0).reshape(2, PW // 2, 2)[:, :, 0]
    factor = jnp.repeat(starts, 2, axis=1)
    diag = jnp.sum(jnp.where(at, inverse_diagonal[:, :, None], 0.0), axis=1)
    side = jnp.sum(jnp.where(at, factor[:, :, None], 0.0), axis=1)
    order_swapped = pivot_order.reshape(2, PW // 2, 2)[:, :, ::-1].reshape(2, PW)
    partner_of = jnp.sum(jnp.where(at, order_swapped[:, :, None], 0), axis=1)
    partner = (jnp.arange(PW, dtype=jnp.int32)[None, :, None] == partner_of[:, None, :]).astype(BF16)
    return partner, diag, side


def smem():
    return pl.BlockSpec(memory_space=pltpu.SMEM)


def vmem():
    return pl.BlockSpec(memory_space=pltpu.VMEM)


def steps(
    front_base, traces, adjacency, pivot_order, pivot_kind, inverse_diagonal, inverse_coupling, readers,
):
    r = lax.axis_index("row")
    c = lax.axis_index("col")
    place = jnp.stack([r, c]).astype(jnp.int32)
    adj = adjacency.reshape(-1)
    own = traces[:, 0]
    base = front_base.reshape(8, 8 * NB, NB)

    mine = lax.dynamic_slice_in_dim(own.reshape(32, 3, NB, NB), 2 * c, 2, axis=0)
    mine_x = lax.ppermute(mine, "row", SWAP_X)
    faces = lax.all_gather(jnp.stack([mine, mine_x]), "row", axis=0, axis_index_groups=Z_LINES)

    chunk = (r // 2 + c // 2) % 8 + 8 * (c % 2)
    low = lax.dynamic_index_in_dim(own[0].reshape(N, 96, NB), chunk, 0, keepdims=False)
    low_a = lax.ppermute(low, BOTH, LOW_A)
    low_b = lax.ppermute(low, BOTH, LOW_B)
    low = jnp.where(c < 8, low_a, low_b)
    low_faces = lax.all_to_all(jnp.broadcast_to(low[None], (N, 96, NB)), "row", 0, 0, tiled=True)

    base_low = front_base[:, 0, :, 0, 0, :]
    base_far = lax.ppermute(jnp.concatenate([base_low[4:], base_low[:1]]), "col", HALVE)
    half, first = pl.pallas_call(
        panel_block_kernel,
        out_shape=(jax.ShapeDtypeStruct((4, NB, NB), BF16), jax.ShapeDtypeStruct((1, NB // 2, NB), BF16)),
        in_specs=[smem(), smem(), vmem(), vmem(), vmem()],
        out_specs=(vmem(), vmem()),
        scratch_shapes=[pltpu.VMEM((5, NB, NB), F32)],
        name="panel_block",
    )(place, adj, jnp.where(c < 8, jnp.concatenate([base_low[:4], base_low[:1]]), base_far), own, low_faces)

    spread = lax.ppermute(half, BOTH, SPREAD)
    other = lax.ppermute(spread, "row", SWAP_X)
    pair = jnp.stack([spread, other])
    col_half = lax.all_gather(pair, "row", axis=0, axis_index_groups=Z_LINES)

    cross_row = lax.all_to_all(jnp.broadcast_to(first, (N, NB // 2, NB)), "row", 0, 0, tiled=True)[4:8]

    cross_row = cross_row.reshape(1, 2, NB, NB)
    row_own = lax.all_to_all(
        jnp.concatenate([jnp.broadcast_to(half[None], (8, 4, NB, NB)), jnp.broadcast_to(cross_row, (8, 2, NB, NB))], 1),
        "col",
        0,
        0,
        tiled=True,
        axis_index_groups=SAME_CORE,
    )
    row_other = lax.ppermute(row_own, "col", SWAP_CORE)

    partner, diag, side = pivot_tables(pivot_order, pivot_kind, inverse_diagonal, inverse_coupling)

    couplings = pl.pallas_call(
        couple_kernel,
        out_shape=jax.ShapeDtypeStruct((N, 2, NB, NB), BF16),
        in_specs=[smem(), smem(), vmem(), vmem()],
        out_specs=vmem(),
        name="couple",
    )(place, adj, own, faces)
    couplings = lax.all_to_all(couplings, "col", 0, 0, tiled=True)

    front = pl.pallas_call(
        assemble_kernel,
        grid=(8,),
        out_shape=jax.ShapeDtypeStruct((8, 8 * NB, NB), F32),
        in_specs=[
            smem(),
            pl.BlockSpec((1, 8 * NB, NB), lambda a: (a, 0, 0)),
            pl.BlockSpec((1, 4, 3, NB, NB), lambda a: (a, 0, 0, 0, 0)),
        ],
        out_specs=pl.BlockSpec((1, 8 * NB, NB), lambda a: (a, 0, 0)),
        name="assemble",
    )(place, base, own)

    by_two = pl.BlockSpec((2 * NB, PW), lambda s: (s, 0))
    w0r, w1r, cross = pl.pallas_call(
        row_side_kernel,
        grid=(4,),
        out_shape=(jax.ShapeDtypeStruct((8 * NB, PW), BF16),) * 2 + (jax.ShapeDtypeStruct((PW, PW), BF16),),
        in_specs=[smem(), smem(), vmem(), vmem(), vmem(), vmem(), vmem()],
        out_specs=(by_two, by_two, pl.BlockSpec((PW, PW), lambda s: (0, 0))),
        scratch_shapes=[pltpu.VMEM((2 * NB, PW), BF16), pltpu.VMEM((2 * NB, PW), BF16)],
        name="row_side",
    )(place, readers.reshape(-1), row_own, row_other, partner, diag, side)

    out = pl.pallas_call(
        update_kernel,
        grid=(2,),
        out_shape=jax.ShapeDtypeStruct((8, 8 * NB, NB), F32),
        in_specs=[
            smem(),
            smem(),
            smem(),
            pl.BlockSpec((4, 8 * NB, NB), lambda s: (s, 0, 0)),
            vmem(),
            pl.BlockSpec((4 * NB, PW), lambda s: (s, 0)),
            pl.BlockSpec((4 * NB, PW), lambda s: (s, 0)),
            vmem(),
            vmem(),
            vmem(),
            vmem(),
            vmem(),
        ],
        out_specs=pl.BlockSpec((4, 8 * NB, NB), lambda s: (s, 0, 0)),
        scratch_shapes=[pltpu.VMEM((8 * NB, PW), BF16), pltpu.VMEM((8 * NB, PW), BF16)],
        name="update",
    )(place, adj, readers.reshape(-1), front, couplings, w0r, w1r, cross, col_half, partner, diag, side)
    return out.reshape(8, 1, NB, 8, 1, NB)


def solution(mesh):
    in_specs = (
        P(None, "row", None, None, "col", None),
        P(None, "row", None, None, None, None),
        P(),
        P(),
        P(),
        P(),
        P(),
        P(),
    )
    out_specs = P(None, "row", None, None, "col", None)
    return jax.shard_map(steps, mesh=mesh, in_specs=in_specs, out_specs=out_specs, check_vma=False)
```
